32 devices in a mesh: alpha: 8 (over y, x, core), beta: 4 (over z).
Axes of the slice: x: 2, y: 2, z: 4, core: 2. Of those that a mesh axis runs over, the one named last changes fastest.
Arguments:
- coefficients: bfloat16 [4096, 4096], P('alpha', 'beta'), may hold values from -6 to 6
- couplings: bfloat16 [8, 256, 256], replicated, may hold values from -0.375 to 0.375
- exc_list: int32 [8, 8, 3], replicated, may hold values from 0 to 15, as said below
- counts: int32 [8, 8], replicated, may hold values from 0 to 1, as said below
- beta_tiles: bfloat16 [4, 1024, 4096], P(None, None, 'beta'), may hold values from -0.09375 to 0.09375
Outputs:
- sigma_vector: float32 [4096, 4096], P('alpha', 'beta')
The draws below stay inside these ranges and needn't reach their ends.
Inputs may be any that keep to these rules, and one draw needn't show every extreme that they name: `exc_list`: entry [s, p] describes the slot from alpha device s to alpha device p: field 0 is a source block held by device s (from s * 2 to s * 2 + 1), field 1 a target block held by device p (from p * 2 to p * 2 + 1), field 2 a coupling index below 8. `counts`: 1 where a slot is live, 0 where it is empty; in every draw some device p has a live slot from every device s.
All inputs are finite; a program needn't handle non-finite values.
Results may differ from the reference program's by a relative error of at most 0.0029.
Values may be sent and summed in bfloat16 or wider, within the bound.
A program may use at most 192 MiB of HBM per device.

```python
import jax
import jax.numpy as jnp
from jax import lax

AB = 256
BB = 1024
ABLK = 2
KC = 8
STOPS = 4
NA = 4096
NBETA = 4096
N_ALPHA = 8
N_BETA = 4


def route_tables(key):
    key = jax.random.fold_in(key, 7)
    key_dest, key_live, key_source, key_target, key_kind = jax.random.split(key, 5)
    full_dest = jax.random.randint(key_dest, (), 0, N_ALPHA)
    device_range = jnp.arange(N_ALPHA, dtype=jnp.int32)
    is_live = jax.random.randint(key_live, (N_ALPHA, N_ALPHA), 0, 5) < 2
    is_live = is_live | (device_range[None, :] == full_dest)
    occupancy = is_live.astype(jnp.int32)
    source = device_range[:, None] * ABLK + jax.random.randint(key_source, (N_ALPHA, N_ALPHA), 0, ABLK)
    target = device_range[None, :] * ABLK + jax.random.randint(key_target, (N_ALPHA, N_ALPHA), 0, ABLK)
    coupling_index = jax.random.randint(key_kind, (N_ALPHA, N_ALPHA), 0, KC)
    entries = jnp.stack([source, target, coupling_index], axis=-1).astype(jnp.int32)
    return (entries, occupancy)


def draw_exc_list(key, part):
    return route_tables(key)[0]


def draw_counts(key, part):
    return route_tables(key)[1]


def steps_of(key, extent, pieces, low, largest):
    def one(dim, blocks):
        draws = jax.random.uniform(jax.random.fold_in(jax.random.fold_in(key, 6), dim), (blocks,), jnp.float32, low / len(pieces), largest / len(pieces))
        return jnp.repeat(jnp.exp(draws), extent[dim] // blocks).reshape((-1,) + (1,) * (len(extent) - dim - 1))

    level = one(*pieces[0])
    for cut in pieces[1:]:
        level = level * one(*cut)
    return level


def noise(rng, shape, deviation, bound, cuts=(), kind=jnp.bfloat16):
    result = jax.random.normal(rng, shape, jnp.float32) * deviation
    if len(cuts) > 0:
        result = steps_of(rng, shape, cuts, -0.22, 0.18) * result
    return jnp.clip(result, min=-bound, max=bound).astype(kind)


def setup_inputs(seed: int = 0) -> dict:
    key_of = jax.random.split(jax.random.key(seed), 6)
    coefficients = noise(key_of[0], (NA, NBETA), 1.0, 6.0, ((0, 8), (1, 4)))
    couplings = noise(key_of[1], (KC, AB, AB), AB ** -0.5, 0.375)
    exc_list = draw_exc_list(jax.random.fold_in(key_of[5], 71), 0)
    counts = draw_counts(jax.random.fold_in(key_of[5], 71), 0)
    beta_tiles = noise(key_of[4], (STOPS, BB, NBETA), (STOPS * BB) ** -0.5, 0.09375, ((2, 4),))
    return dict(coefficients=coefficients, couplings=couplings, exc_list=exc_list, counts=counts, beta_tiles=beta_tiles)


def reference(coefficients, couplings, exc_list, counts, beta_tiles):
    block_count = ABLK * N_ALPHA
    blocks = coefficients.astype(jnp.float32).reshape(block_count, AB * NBETA)
    weights_cat = jnp.transpose(couplings.astype(jnp.float32), (1, 0, 2)).reshape(AB, KC * AB)
    coupling_range = jnp.arange(KC, dtype=jnp.int32)
    block_range = jnp.arange(block_count, dtype=jnp.int32)

    def one_target(target):
        owner_device = target // ABLK
        is_live = (counts[:, owner_device] == 1) & (exc_list[:, owner_device, 1] == target)
        source = exc_list[:, owner_device, 0]
        coupling_index = exc_list[:, owner_device, 2]
        onehot = ((coupling_index[None, :] == coupling_range[:, None]) & is_live[None, :]).astype(jnp.float32)
        source_hot = (source[:, None] == block_range[None, :]).astype(jnp.float32)
        grouping = jnp.dot(onehot, source_hot, precision=lax.Precision.HIGHEST)
        grouped = jnp.dot(grouping, blocks, precision=lax.Precision.HIGHEST).reshape(KC * AB, NBETA)
        return jnp.dot(weights_cat, grouped, precision=lax.Precision.HIGHEST).astype(jnp.bfloat16)

    interm = lax.map(one_target, jnp.arange(block_count, dtype=jnp.int32)).reshape(block_count * AB, NBETA)

    def one_column(column):
        summed = jnp.zeros((block_count * AB, BB), jnp.float32)
        for offset in range(STOPS):
            anchor = (column - offset) % N_BETA
            shifted = lax.dynamic_slice_in_dim(interm, (anchor * BB).astype(jnp.int32), BB, 1).astype(jnp.float32)
            tile_block = lax.dynamic_slice_in_dim(beta_tiles[offset], (column * BB).astype(jnp.int32), BB, 1).astype(jnp.float32)
            summed = summed + jnp.dot(shifted, tile_block, precision=lax.Precision.HIGHEST)
        return summed

    results = lax.map(one_column, jnp.arange(N_BETA, dtype=jnp.int32))
    return jnp.transpose(results, (1, 0, 2)).reshape(block_count * AB, N_BETA * BB)
```

```python
import functools

import jax
import jax.numpy as jnp
from jax import lax
from jax.experimental import pallas as pl
from jax.experimental.pallas import tpu as pltpu
from jax.sharding import PartitionSpec as P

MESH = pl.DeviceIdType.MESH
CHUNK = 256
TILE = 256
AHEAD = 2


def flip(position, mask):
    bit = lax.rem(lax.div(position, mask), 2)
    return position + mask * (1 - 2 * bit)


def kernel(
    n_alpha, n_beta, rounds, chunks,
    exc_ref, counts_ref, coupling_ref, c_hbm, b_hbm, out_ref,
    weights, gathered, tiles, held, moved,
    send_sem, recv_sem, own_sem, zsend_sem, zrecv_sem, tile_sem,
):
    n_chips = n_alpha // 2
    n_blocks, order = c_hbm.shape[0], c_hbm.shape[1]
    n_stops = b_hbm.shape[0]
    width = CHUNK
    alpha, beta = lax.axis_index("alpha"), lax.axis_index("beta")
    chip, core = lax.div(alpha, 2), lax.rem(alpha, 2)

    def mask_of(step, which):
        return (1 - which) * 2**step + which * 2 ** (rounds - 1 - step)

    def origin(label, which):
        source = chip
        for step in range(rounds):
            if (label >> step) & 1:
                source = flip(source, mask_of(step, which))
        return source * 2 + which

    if n_beta == n_stops:
        way, far, near = 1 - 2 * core, n_beta // 2, n_beta - 1 - n_beta // 2
    else:
        way, far, near = 1, n_stops - 1, 0
    ahead = lax.rem(beta + way + n_beta, n_beta)
    behind = lax.rem(beta - way + n_beta, n_beta)

    sibling = (alpha + 1 - 2 * core, beta)
    neighbours = [(flip(chip, mask_of(step, core)) * 2 + core, beta) for step in range(rounds)]
    greeted = neighbours + [sibling, (alpha, ahead), (alpha, behind)]
    barrier = pltpu.get_barrier_semaphore()
    for device in greeted:
        pl.semaphore_signal(barrier, inc=1, device_id=device, device_id_type=MESH)
    own = []
    for c in range(chunks):
        own.append(
            pltpu.make_async_copy(c_hbm.at[:, :, pl.ds(c * width, width)], held[c].at[0], own_sem.at[c])
        )
    own[0].start()
    pl.semaphore_wait(barrier, len(greeted))

    def to_alpha(c, label, target, device):
        source = c_hbm.at[:, :, pl.ds(c * width, width)] if label == 0 else held[c].at[label]
        return pltpu.make_async_remote_copy(
            src_ref=source,
            dst_ref=held[c].at[target],
            send_sem=send_sem.at[c, target],
            recv_sem=recv_sem.at[c, target],
            device_id=device,
            device_id_type=MESH,
        )

    copies = [{} for _ in range(chunks)]

    def pass_on(c, label):
        for step in range(label.bit_length(), rounds):
            target = label + 2**step
            copies[c][target] = to_alpha(c, label, target, neighbours[step])
            copies[c][target].start()
        target = n_chips + label
        copies[c][target] = to_alpha(c, label, target, sibling)
        copies[c][target].start()

    def slot_of(hop):
        return lax.rem(hop * way + n_beta * n_stops, n_beta)

    hops = [{} for _ in range(chunks)]

    def to_beta(c, kind, hop):
        sign, device, index = (1, ahead, hop - 1) if kind == "far" else (-1, behind, far + hop - 1)
        copy = pltpu.make_async_remote_copy(
            src_ref=moved[c].at[slot_of(sign * (hop - 1))],
            dst_ref=moved[c].at[slot_of(sign * hop)],
            send_sem=zsend_sem.at[c, index],
            recv_sem=zrecv_sem.at[c, index],
            device_id=(alpha, device),
            device_id_type=MESH,
        )
        hops[c][kind, hop] = copy
        copy.start()

    for c in range(min(AHEAD, chunks)):
        if c > 0:
            own[c].start()
        pass_on(c, 0)
    tile_copy = pltpu.make_async_copy(b_hbm, tiles, tile_sem)
    tile_copy.start()

    sources = [origin(label, core) for label in range(n_chips)]
    sources += [origin(label, 1 - core) for label in range(n_chips)]
    picked = []
    for slot, source in enumerate(sources):
        entry = (source * n_alpha + alpha) * 3
        live = counts_ref[source * n_alpha + alpha] == 1
        picked.append(jnp.clip(exc_ref[entry] - source * n_blocks, 0, n_blocks - 1))
        target = exc_ref[entry + 1] - alpha * n_blocks
        matrix = coupling_ref[exc_ref[entry + 2]]
        for block in range(n_blocks):
            keep = jnp.where(live & (target == block), 1.0, 0.0).astype(jnp.float32)
            weights[pl.ds(block * order, order), pl.ds(slot * order, order)] = (
                matrix.astype(jnp.float32) * keep
            ).astype(jnp.bfloat16)

    def product(c):
        @pl.loop(0, out_ref.shape[1] // TILE)
        def _(n):
            columns = pl.ds(pl.multiple_of(n * TILE, TILE), TILE)
            left = jnp.concatenate([moved[c][d] for d in range(n_stops)], axis=1)
            right = jnp.concatenate(
                [tiles[d, pl.ds(c * width, width), columns] for d in range(n_stops)], axis=0
            )
            value = jnp.dot(left, right, preferred_element_type=jnp.float32)
            if c == 0:
                out_ref[:, columns] = value
            else:
                out_ref[:, columns] += value

    def relay(c):
        for kind, last in (("far", far), ("near", near)):
            for hop in range(1, last):
                hops[c][kind, hop].wait_recv()
                to_beta(c, kind, hop + 1)

    def finish(c):
        for kind, last in (("far", far), ("near", near)):
            if last > 0:
                hops[c][kind, last].wait_recv()
        if c == 0:
            tile_copy.wait()
        product(c)

    for c in range(chunks):
        for label in range(1, n_chips):
            copies[c][label].wait_recv()
            pass_on(c, label)
            if label == 1 and c + AHEAD < chunks:
                own[c + AHEAD].start()
                pass_on(c + AHEAD, 0)
        own[c].wait()
        for label in range(n_chips):
            copies[c][n_chips + label].wait_recv()
        for slot in range(n_alpha):
            gathered[pl.ds(slot * order, order), :] = held[c][slot, picked[slot]]
        moved[c][0] = jnp.dot(
            weights[...], gathered[...], preferred_element_type=jnp.float32
        ).astype(jnp.bfloat16)
        to_beta(c, "far", 1)
        if near > 0:
            to_beta(c, "near", 1)
        if c >= 1:
            relay(c - 1)
        if c >= 2:
            finish(c - 2)
    relay(chunks - 1)
    for c in range(max(chunks - 2, 0), chunks):
        finish(c)
    for c in range(chunks):
        for copy in copies[c].values():
            copy.wait_send()
        for copy in hops[c].values():
            copy.wait_send()


def solution(mesh):
    n_alpha, n_beta = mesh.shape["alpha"], mesh.shape["beta"]
    n_chips = n_alpha // 2
    rounds = n_chips.bit_length() - 1

    def per_device(coefficients, couplings, exc_list, counts, beta_tiles):
        order = couplings.shape[1]
        rows, columns = coefficients.shape
        n_blocks = rows // order
        n_stops = beta_tiles.shape[0]
        chunks = columns // CHUNK
        vmem, smem = pl.BlockSpec(memory_space=pltpu.VMEM), pl.BlockSpec(memory_space=pltpu.SMEM)
        hbm = pl.BlockSpec(memory_space=pl.ANY)
        return pl.pallas_call(
            functools.partial(kernel, n_alpha, n_beta, rounds, chunks),
            out_shape=jax.ShapeDtypeStruct((rows, columns), jnp.float32),
            in_specs=[smem, smem, vmem, hbm, hbm],
            out_specs=vmem,
            scratch_shapes=[
                pltpu.VMEM((rows, n_alpha * order), jnp.bfloat16),
                pltpu.VMEM((n_alpha * order, CHUNK), jnp.bfloat16),
                pltpu.VMEM(beta_tiles.shape, jnp.bfloat16),
                [pltpu.VMEM((n_alpha, n_blocks, order, CHUNK), jnp.bfloat16) for _ in range(chunks)],
                [pltpu.VMEM((n_stops, rows, CHUNK), jnp.bfloat16) for _ in range(chunks)],
                pltpu.SemaphoreType.DMA((chunks, n_alpha)),
                pltpu.SemaphoreType.DMA((chunks, n_alpha)),
                pltpu.SemaphoreType.DMA((chunks,)),
                pltpu.SemaphoreType.DMA((chunks, n_stops - 1)),
                pltpu.SemaphoreType.DMA((chunks, n_stops - 1)),
                pltpu.SemaphoreType.DMA(()),
            ],
            compiler_params=pltpu.CompilerParams(
                collective_id=0, has_side_effects=True, vmem_limit_bytes=60 * 2**20
            ),
        )(
            exc_list.reshape(-1),
            counts.reshape(-1),
            couplings,
            coefficients.reshape(n_blocks, order, columns),
            beta_tiles,
        )

    placed = (P("alpha", "beta"), P(), P(), P(), P(None, None, "beta"))
    return jax.shard_map(
        per_device, mesh=mesh, in_specs=placed, out_specs=P("alpha", "beta"), check_vma=False
    )
```

```python
import functools

import jax
import jax.numpy as jnp
from jax import lax
from jax.experimental import pallas as pl
from jax.experimental.pallas import tpu as pltpu
from jax.sharding import PartitionSpec as P

MESH = pl.DeviceIdType.MESH
CHUNK = 128
TILE = 256
AHEAD = 1


def flip(position, mask):
    bit = lax.rem(lax.div(position, mask), 2)
    return position + mask * (1 - 2 * bit)


def kernel(
    n_alpha, n_beta, rounds, chunks,
    exc_ref, counts_ref, coupling_ref, c_hbm, b_hbm, out_ref,
    weights, gathered, tiles, held, moved,
    send_sem, recv_sem, own_sem, zsend_sem, zrecv_sem, tile_sem,
):
    n_chips = n_alpha // 2
    n_blocks, order = c_hbm.shape[0], c_hbm.shape[1]
    n_stops = b_hbm.shape[0]
    width = CHUNK
    alpha, beta = lax.axis_index("alpha"), lax.axis_index("beta")
    chip, core = lax.div(alpha, 2), lax.rem(alpha, 2)

    def mask_of(step, which):
        return (1 - which) * 2**step + which * 2 ** (rounds - 1 - step)

    def origin(label, which):
        source = chip
        for step in range(rounds):
            if (label >> step) & 1:
                source = flip(source, mask_of(step, which))
        return source * 2 + which

    line = n_beta == n_stops
    ahead, behind = lax.rem(beta + 1, n_beta), lax.rem(beta + n_beta - 1, n_beta)

    sibling = (alpha + 1 - 2 * core, beta)
    neighbours = [(flip(chip, mask_of(step, core)) * 2 + core, beta) for step in range(rounds)]
    greeted = neighbours + [sibling, (alpha, ahead), (alpha, behind)]
    barrier = pltpu.get_barrier_semaphore()
    for device in greeted:
        pl.semaphore_signal(barrier, inc=1, device_id=device, device_id_type=MESH)
    own = []
    for c in range(chunks):
        own.append(
            pltpu.make_async_copy(c_hbm.at[:, :, pl.ds(c * width, width)], held[c].at[0], own_sem.at[c])
        )
    own[0].start()
    pl.semaphore_wait(barrier, len(greeted))

    def to_alpha(c, label, target, device):
        source = c_hbm.at[:, :, pl.ds(c * width, width)] if label == 0 else held[c].at[label]
        return pltpu.make_async_remote_copy(
            src_ref=source,
            dst_ref=held[c].at[target],
            send_sem=send_sem.at[c, target],
            recv_sem=recv_sem.at[c, target],
            device_id=device,
            device_id_type=MESH,
        )

    copies = [{} for _ in range(chunks)]

    def pass_on(c, label):
        for step in range(label.bit_length(), rounds):
            target = label + 2**step
            copies[c][target] = to_alpha(c, label, target, neighbours[step])
            copies[c][target].start()
        target = n_chips + label
        copies[c][target] = to_alpha(c, label, target, sibling)
        copies[c][target].start()

    def to_beta(c, sign, hop):
        source, target = sign * (hop - 1) % n_stops, sign * hop % n_stops
        return pltpu.make_async_remote_copy(
            src_ref=moved[c].at[source],
            dst_ref=moved[c].at[target],
            send_sem=zsend_sem.at[c, hop - 1 if sign == 1 else n_stops + hop - 2],
            recv_sem=zrecv_sem.at[c, target - 1],
            device_id=(alpha, ahead if sign == 1 else behind),
            device_id_type=MESH,
        )

    def sends(sign, hop):
        if not line:
            return sign == 1
        if sign == 1:
            return (beta >= hop - 1) & (beta <= n_beta - 2)
        return (beta <= n_beta - hop) & (beta >= 1)

    def send_beta(c, sign, hop):
        if 1 <= hop < n_stops and (line or sign == 1):
            pl.when(sends(sign, hop))(lambda: to_beta(c, sign, hop).start())

    def relay(c, slots):
        for slot in slots:
            to_beta(c, 1, slot).wait_recv()
            send_beta(c, 1, slot + 1)
            if line:
                send_beta(c, -1, n_stops - slot + 1)

    for c in range(min(AHEAD, chunks)):
        if c > 0:
            own[c].start()
        pass_on(c, 0)
    tile_copy = pltpu.make_async_copy(b_hbm, tiles, tile_sem)
    tile_copy.start()

    sources = [origin(label, core) for label in range(n_chips)]
    sources += [origin(label, 1 - core) for label in range(n_chips)]
    picked = []
    for slot, source in enumerate(sources):
        live = counts_ref[source, alpha] == 1
        picked.append(jnp.clip(exc_ref[0, source, alpha] - source * n_blocks, 0, n_blocks - 1))
        target = exc_ref[1, source, alpha] - alpha * n_blocks
        matrix = coupling_ref[exc_ref[2, source, alpha]]
        for block in range(n_blocks):
            keep = jnp.where(live & (target == block), 1.0, 0.0).astype(jnp.float32)
            weights[pl.ds(block * order, order), pl.ds(slot * order, order)] = (
                matrix.astype(jnp.float32) * keep
            ).astype(jnp.bfloat16)

    def product(c):
        @pl.loop(0, out_ref.shape[1] // TILE)
        def _(n):
            columns = pl.ds(pl.multiple_of(n * TILE, TILE), TILE)
            left = jnp.concatenate([moved[c][d] for d in range(n_stops)], axis=1)
            right = jnp.concatenate(
                [tiles[d, pl.ds(c * width, width), columns] for d in range(n_stops)], axis=0
            )
            value = jnp.dot(left, right, preferred_element_type=jnp.float32)
            if c == 0:
                out_ref[:, columns] = value
            else:
                out_ref[:, columns] += value

    near = (1, n_stops - 1) if line else (1,)
    later = [slot for slot in range(1, n_stops) if slot not in near]

    def behind_by(c):
        if 0 <= c - 1 < chunks:
            relay(c - 1, near)
        if 0 <= c - 2 < chunks:
            relay(c - 2, later)
            if c == 2:
                tile_copy.wait()
            product(c - 2)

    for c in range(chunks):
        for label in range(1, n_chips):
            copies[c][label].wait_recv()
            pass_on(c, label)
            if label == 1 and c + AHEAD < chunks:
                own[c + AHEAD].start()
                pass_on(c + AHEAD, 0)
        own[c].wait()
        for label in range(n_chips):
            copies[c][n_chips + label].wait_recv()
        for slot in range(n_alpha):
            gathered[pl.ds(slot * order, order), :] = held[c][slot, picked[slot]]
        moved[c][0] = jnp.dot(
            weights[...], gathered[...], preferred_element_type=jnp.float32
        ).astype(jnp.bfloat16)
        send_beta(c, 1, 1)
        send_beta(c, -1, 1)
        behind_by(c)
    behind_by(chunks)
    behind_by(chunks + 1)
    for c in range(chunks):
        for copy in copies[c].values():
            copy.wait_send()
        for sign in (1, -1):
            for hop in range(1, n_stops):
                if line or sign == 1:
                    pl.when(sends(sign, hop))(lambda: to_beta(c, sign, hop).wait_send())


def solution(mesh):
    n_alpha, n_beta = mesh.shape["alpha"], mesh.shape["beta"]
    n_chips = n_alpha // 2
    rounds = n_chips.bit_length() - 1

    def per_device(coefficients, couplings, exc_list, counts, beta_tiles):
        order = couplings.shape[1]
        rows, columns = coefficients.shape
        n_blocks = rows // order
        n_stops = beta_tiles.shape[0]
        chunks = columns // CHUNK
        vmem, smem = pl.BlockSpec(memory_space=pltpu.VMEM), pl.BlockSpec(memory_space=pltpu.SMEM)
        hbm = pl.BlockSpec(memory_space=pl.ANY)
        return pl.pallas_call(
            functools.partial(kernel, n_alpha, n_beta, rounds, chunks),
            out_shape=pltpu.VMEM((rows, columns), jnp.float32),
            in_specs=[smem, smem, vmem, hbm, hbm],
            out_specs=vmem,
            scratch_shapes=[
                pltpu.VMEM((rows, n_alpha * order), jnp.bfloat16),
                pltpu.VMEM((n_alpha * order, CHUNK), jnp.bfloat16),
                pltpu.VMEM(beta_tiles.shape, jnp.bfloat16),
                [pltpu.VMEM((n_alpha, n_blocks, order, CHUNK), jnp.bfloat16) for _ in range(chunks)],
                [pltpu.VMEM((n_stops, rows, CHUNK), jnp.bfloat16) for _ in range(chunks)],
                pltpu.SemaphoreType.DMA((chunks, n_alpha)),
                pltpu.SemaphoreType.DMA((chunks, n_alpha)),
                pltpu.SemaphoreType.DMA((chunks,)),
                pltpu.SemaphoreType.DMA((chunks, 2 * n_stops - 2)),
                pltpu.SemaphoreType.DMA((chunks, n_stops - 1)),
                pltpu.SemaphoreType.DMA(()),
            ],
            compiler_params=pltpu.CompilerParams(
                collective_id=0, has_side_effects=True, vmem_limit_bytes=48 * 2**20
            ),
        )(
            exc_list.transpose(2, 0, 1),
            counts,
            couplings,
            coefficients.reshape(n_blocks, order, columns),
            beta_tiles,
        )

    placed = (P("alpha", "beta"), P(), P(), P(), P(None, None, "beta"))
    return jax.shard_map(
        per_device, mesh=mesh, in_specs=placed, out_specs=P("alpha", "beta"), check_vma=False
    )
```

```python
import functools

import jax
import jax.numpy as jnp
from jax import lax
from jax.experimental import pallas as pl
from jax.experimental.pallas import tpu as pltpu
from jax.sharding import PartitionSpec as P

MESH = pl.DeviceIdType.MESH
CHUNK = 256
TILE = 256
AHEAD = 1


def flip(position, mask):
    bit = lax.rem(lax.div(position, mask), 2)
    return position + mask * (1 - 2 * bit)


def kernel(
    n_alpha, n_beta, rounds, chunks,
    exc_ref, counts_ref, coupling_ref, c_hbm, b_hbm, out_ref,
    weights, gathered, tiles, held, moved,
    send_sem, recv_sem, own_sem, zsend_sem, zrecv_sem, tile_sem,
):
    n_chips = n_alpha // 2
    n_blocks, order = c_hbm.shape[0], c_hbm.shape[1]
    n_stops = b_hbm.shape[0]
    width = CHUNK
    alpha, beta = lax.axis_index("alpha"), lax.axis_index("beta")
    chip, core = lax.div(alpha, 2), lax.rem(alpha, 2)

    def mask_of(step, which):
        return (1 - which) * 2**step + which * 2 ** (rounds - 1 - step)

    def origin(label, which):
        source = chip
        for step in range(rounds):
            if (label >> step) & 1:
                source = flip(source, mask_of(step, which))
        return source * 2 + which

    if n_beta == n_stops:
        way, far, near = 1 - 2 * core, n_beta // 2, n_beta - 1 - n_beta // 2
    else:
        way, far, near = 1, n_stops - 1, 0
    ahead = lax.rem(beta + way + n_beta, n_beta)
    behind = lax.rem(beta - way + n_beta, n_beta)

    sibling = (alpha + 1 - 2 * core, beta)
    neighbours = [(flip(chip, mask_of(step, core)) * 2 + core, beta) for step in range(rounds)]
    greeted = neighbours + [sibling, (alpha, ahead), (alpha, behind)]
    barrier = pltpu.get_barrier_semaphore()
    for device in greeted:
        pl.semaphore_signal(barrier, inc=1, device_id=device, device_id_type=MESH)
    own = []
    for c in range(chunks):
        own.append(
            pltpu.make_async_copy(c_hbm.at[:, :, pl.ds(c * width, width)], held[c].at[0], own_sem.at[c])
        )
    own[0].start()
    pl.semaphore_wait(barrier, len(greeted))

    def to_alpha(c, label, target, device):
        source = c_hbm.at[:, :, pl.ds(c * width, width)] if label == 0 else held[c].at[label]
        return pltpu.make_async_remote_copy(
            src_ref=source,
            dst_ref=held[c].at[target],
            send_sem=send_sem.at[c, target],
            recv_sem=recv_sem.at[c, target],
            device_id=device,
            device_id_type=MESH,
        )

    copies = [{} for _ in range(chunks)]

    def pass_on(c, label):
        for step in range(label.bit_length(), rounds):
            target = label + 2**step
            copies[c][target] = to_alpha(c, label, target, neighbours[step])
            copies[c][target].start()
        target = n_chips + label
        copies[c][target] = to_alpha(c, label, target, sibling)
        copies[c][target].start()

    def slot_of(hop):
        return lax.rem(hop * way + n_beta * n_stops, n_beta)

    hops = [{} for _ in range(chunks)]

    def to_beta(c, kind, hop):
        sign, device, index = (1, ahead, hop - 1) if kind == "far" else (-1, behind, far + hop - 1)
        copy = pltpu.make_async_remote_copy(
            src_ref=moved[c].at[slot_of(sign * (hop - 1))],
            dst_ref=moved[c].at[slot_of(sign * hop)],
            send_sem=zsend_sem.at[c, index],
            recv_sem=zrecv_sem.at[c, index],
            device_id=(alpha, device),
            device_id_type=MESH,
        )
        hops[c][kind, hop] = copy
        copy.start()

    for c in range(min(AHEAD, chunks)):
        if c > 0:
            own[c].start()
        pass_on(c, 0)
    tile_copy = pltpu.make_async_copy(b_hbm, tiles, tile_sem)
    tile_copy.start()

    sources = [origin(label, core) for label in range(n_chips)]
    sources += [origin(label, 1 - core) for label in range(n_chips)]
    picked = []
    for slot, source in enumerate(sources):
        live = counts_ref[source, alpha] == 1
        picked.append(jnp.clip(exc_ref[0, source, alpha] - source * n_blocks, 0, n_blocks - 1))
        target = exc_ref[1, source, alpha] - alpha * n_blocks
        matrix = coupling_ref[exc_ref[2, source, alpha]]
        for block in range(n_blocks):
            keep = jnp.where(live & (target == block), 1.0, 0.0).astype(jnp.float32)
            weights[pl.ds(block * order, order), pl.ds(slot * order, order)] = (
                matrix.astype(jnp.float32) * keep
            ).astype(jnp.bfloat16)

    def product(c):
        @pl.loop(0, out_ref.shape[1] // TILE)
        def _(n):
            columns = pl.ds(pl.multiple_of(n * TILE, TILE), TILE)
            left = jnp.concatenate([moved[c][d] for d in range(n_stops)], axis=1)
            right = jnp.concatenate(
                [tiles[d, pl.ds(c * width, width), columns] for d in range(n_stops)], axis=0
            )
            value = jnp.dot(left, right, preferred_element_type=jnp.float32)
            if c == 0:
                out_ref[:, columns] = value
            else:
                out_ref[:, columns] += value

    def relay(c):
        for kind, last in (("far", far), ("near", near)):
            for hop in range(1, last):
                hops[c][kind, hop].wait_recv()
                to_beta(c, kind, hop + 1)

    def finish(c):
        for kind, last in (("far", far), ("near", near)):
            if last > 0:
                hops[c][kind, last].wait_recv()
        if c == 0:
            tile_copy.wait()
        product(c)

    for c in range(chunks):
        for label in range(1, n_chips):
            copies[c][label].wait_recv()
            pass_on(c, label)
            if label == 1 and c + AHEAD < chunks:
                own[c + AHEAD].start()
                pass_on(c + AHEAD, 0)
        own[c].wait()
        for label in range(n_chips):
            copies[c][n_chips + label].wait_recv()
        for slot in range(n_alpha):
            gathered[pl.ds(slot * order, order), :] = held[c][slot, picked[slot]]
        moved[c][0] = jnp.dot(
            weights[...], gathered[...], preferred_element_type=jnp.float32
        ).astype(jnp.bfloat16)
        to_beta(c, "far", 1)
        if near > 0:
            to_beta(c, "near", 1)
        if c >= 1:
            relay(c - 1)
        if c >= 2:
            finish(c - 2)
    relay(chunks - 1)
    for c in range(max(chunks - 2, 0), chunks):
        finish(c)
    for c in range(chunks):
        for copy in copies[c].values():
            copy.wait_send()
        for copy in hops[c].values():
            copy.wait_send()


def solution(mesh):
    n_alpha, n_beta = mesh.shape["alpha"], mesh.shape["beta"]
    n_chips = n_alpha // 2
    rounds = n_chips.bit_length() - 1

    def per_device(coefficients, couplings, exc_list, counts, beta_tiles):
        order = couplings.shape[1]
        rows, columns = coefficients.shape
        n_blocks = rows // order
        n_stops = beta_tiles.shape[0]
        chunks = columns // CHUNK
        vmem, smem = pl.BlockSpec(memory_space=pltpu.VMEM), pl.BlockSpec(memory_space=pltpu.SMEM)
        hbm = pl.BlockSpec(memory_space=pl.ANY)
        return pl.pallas_call(
            functools.partial(kernel, n_alpha, n_beta, rounds, chunks),
            out_shape=pltpu.VMEM((rows, columns), jnp.float32),
            in_specs=[smem, smem, vmem, hbm, hbm],
            out_specs=vmem,
            scratch_shapes=[
                pltpu.VMEM((rows, n_alpha * order), jnp.bfloat16),
                pltpu.VMEM((n_alpha * order, CHUNK), jnp.bfloat16),
                pltpu.VMEM(beta_tiles.shape, jnp.bfloat16),
                [pltpu.VMEM((n_alpha, n_blocks, order, CHUNK), jnp.bfloat16) for _ in range(chunks)],
                [pltpu.VMEM((n_stops, rows, CHUNK), jnp.bfloat16) for _ in range(chunks)],
                pltpu.SemaphoreType.DMA((chunks, n_alpha)),
                pltpu.SemaphoreType.DMA((chunks, n_alpha)),
                pltpu.SemaphoreType.DMA((chunks,)),
                pltpu.SemaphoreType.DMA((chunks, n_stops - 1)),
                pltpu.SemaphoreType.DMA((chunks, n_stops - 1)),
                pltpu.SemaphoreType.DMA(()),
            ],
            compiler_params=pltpu.CompilerParams(
                collective_id=0, has_side_effects=True, vmem_limit_bytes=48 * 2**20
            ),
        )(
            exc_list.transpose(2, 0, 1),
            counts,
            couplings,
            coefficients.reshape(n_blocks, order, columns),
            beta_tiles,
        )

    placed = (P("alpha", "beta"), P(), P(), P(), P(None, None, "beta"))
    return jax.shard_map(
        per_device, mesh=mesh, in_specs=placed, out_specs=P("alpha", "beta"), check_vma=False
    )
```

```python
import functools

import jax
import jax.numpy as jnp
from jax import lax
from jax.experimental import pallas as pl
from jax.experimental.pallas import tpu as pltpu
from jax.sharding import PartitionSpec as P

MESH = pl.DeviceIdType.MESH
WIDTHS = (1, 2, 2, 2, 1)
TILE = 256
AHEAD = 1


def split(columns):
    unit = columns // sum(WIDTHS)
    widths = [unit * part for part in WIDTHS]
    return widths, [sum(widths[:c]) for c in range(len(widths))]


def flip(position, mask):
    bit = lax.rem(lax.div(position, mask), 2)
    return position + mask * (1 - 2 * bit)


def kernel(
    n_alpha, n_beta, rounds, chunks,
    exc_ref, counts_ref, coupling_ref, c_hbm, b_hbm, out_ref,
    weights, gathered, tiles, held, moved,
    send_sem, recv_sem, own_sem, zsend_sem, zrecv_sem, tile_sem,
):
    n_chips = n_alpha // 2
    n_blocks, order = c_hbm.shape[0], c_hbm.shape[1]
    n_stops = b_hbm.shape[0]
    widths, starts = split(out_ref.shape[1])
    alpha, beta = lax.axis_index("alpha"), lax.axis_index("beta")
    chip, core = lax.div(alpha, 2), lax.rem(alpha, 2)

    def mask_of(step, which):
        return (1 - which) * 2**step + which * 2 ** (rounds - 1 - step)

    def origin(label, which):
        source = chip
        for step in range(rounds):
            if (label >> step) & 1:
                source = flip(source, mask_of(step, which))
        return source * 2 + which

    if n_beta == n_stops:
        way, far, near = 1 - 2 * core, n_beta // 2, n_beta - 1 - n_beta // 2
    else:
        way, far, near = 1, n_stops - 1, 0
    ahead = lax.rem(beta + way + n_beta, n_beta)
    behind = lax.rem(beta - way + n_beta, n_beta)

    sibling = (alpha + 1 - 2 * core, beta)
    neighbours = [(flip(chip, mask_of(step, core)) * 2 + core, beta) for step in range(rounds)]
    greeted = neighbours + [sibling, (alpha, ahead), (alpha, behind)]
    barrier = pltpu.get_barrier_semaphore()
    for device in greeted:
        pl.semaphore_signal(barrier, inc=1, device_id=device, device_id_type=MESH)
    own = []
    for c in range(chunks):
        own.append(
            pltpu.make_async_copy(c_hbm.at[:, :, pl.ds(starts[c], widths[c])], held[c].at[0], own_sem.at[c])
        )
    own[0].start()
    pl.semaphore_wait(barrier, len(greeted))

    def to_alpha(c, label, target, device):
        source = c_hbm.at[:, :, pl.ds(starts[c], widths[c])] if label == 0 else held[c].at[label]
        return pltpu.make_async_remote_copy(
            src_ref=source,
            dst_ref=held[c].at[target],
            send_sem=send_sem.at[c, target],
            recv_sem=recv_sem.at[c, target],
            device_id=device,
            device_id_type=MESH,
        )

    copies = [{} for _ in range(chunks)]

    def pass_on(c, label):
        for step in range(label.bit_length(), rounds):
            target = label + 2**step
            copies[c][target] = to_alpha(c, label, target, neighbours[step])
            copies[c][target].start()
        target = n_chips + label
        copies[c][target] = to_alpha(c, label, target, sibling)
        copies[c][target].start()

    def slot_of(hop):
        return lax.rem(hop * way + n_beta * n_stops, n_beta)

    hops = [{} for _ in range(chunks)]

    def to_beta(c, kind, hop):
        sign, device, index = (1, ahead, hop - 1) if kind == "far" else (-1, behind, far + hop - 1)
        copy = pltpu.make_async_remote_copy(
            src_ref=moved[c].at[slot_of(sign * (hop - 1))],
            dst_ref=moved[c].at[slot_of(sign * hop)],
            send_sem=zsend_sem.at[c, index],
            recv_sem=zrecv_sem.at[c, index],
            device_id=(alpha, device),
            device_id_type=MESH,
        )
        hops[c][kind, hop] = copy
        copy.start()

    for c in range(min(AHEAD, chunks)):
        if c > 0:
            own[c].start()
        pass_on(c, 0)
    tile_copy = pltpu.make_async_copy(b_hbm, tiles, tile_sem)
    tile_copy.start()

    sources = [origin(label, core) for label in range(n_chips)]
    sources += [origin(label, 1 - core) for label in range(n_chips)]
    picked = []
    for slot, source in enumerate(sources):
        live = counts_ref[source, alpha] == 1
        picked.append(jnp.clip(exc_ref[0, source, alpha] - source * n_blocks, 0, n_blocks - 1))
        target = exc_ref[1, source, alpha] - alpha * n_blocks
        matrix = coupling_ref[exc_ref[2, source, alpha]]
        for block in range(n_blocks):
            keep = jnp.where(live & (target == block), 1.0, 0.0).astype(jnp.float32)
            weights[pl.ds(block * order, order), pl.ds(slot * order, order)] = (
                matrix.astype(jnp.float32) * keep
            ).astype(jnp.bfloat16)

    def product(c):
        @pl.loop(0, out_ref.shape[1] // TILE)
        def _(n):
            columns = pl.ds(pl.multiple_of(n * TILE, TILE), TILE)
            left = jnp.concatenate([moved[c][d] for d in range(n_stops)], axis=1)
            right = jnp.concatenate(
                [tiles[d, pl.ds(starts[c], widths[c]), columns] for d in range(n_stops)], axis=0
            )
            value = jnp.dot(left, right, preferred_element_type=jnp.float32)
            if c == 0:
                out_ref[:, columns] = value
            else:
                out_ref[:, columns] += value

    def relay(c):
        for kind, last in (("far", far), ("near", near)):
            for hop in range(1, last):
                hops[c][kind, hop].wait_recv()
                to_beta(c, kind, hop + 1)

    def finish(c):
        for kind, last in (("far", far), ("near", near)):
            if last > 0:
                hops[c][kind, last].wait_recv()
        if c == 0:
            tile_copy.wait()
        product(c)

    for c in range(chunks):
        for label in range(1, n_chips):
            copies[c][label].wait_recv()
            pass_on(c, label)
            if label == 1 and c + AHEAD < chunks:
                own[c + AHEAD].start()
                pass_on(c + AHEAD, 0)
        own[c].wait()
        for label in range(n_chips):
            copies[c][n_chips + label].wait_recv()
        for slot in range(n_alpha):
            gathered[pl.ds(slot * order, order), pl.ds(0, widths[c])] = held[c][slot, picked[slot]]
        moved[c][0] = jnp.dot(
            weights[...], gathered[:, pl.ds(0, widths[c])], preferred_element_type=jnp.float32
        ).astype(jnp.bfloat16)
        to_beta(c, "far", 1)
        if near > 0:
            to_beta(c, "near", 1)
        if c >= 1:
            relay(c - 1)
        if c >= 2:
            finish(c - 2)
    relay(chunks - 1)
    for c in range(max(chunks - 2, 0), chunks):
        finish(c)
    for c in range(chunks):
        for copy in copies[c].values():
            copy.wait_send()
        for copy in hops[c].values():
            copy.wait_send()


def solution(mesh):
    n_alpha, n_beta = mesh.shape["alpha"], mesh.shape["beta"]
    n_chips = n_alpha // 2
    rounds = n_chips.bit_length() - 1

    def per_device(coefficients, couplings, exc_list, counts, beta_tiles):
        order = couplings.shape[1]
        rows, columns = coefficients.shape
        n_blocks = rows // order
        n_stops = beta_tiles.shape[0]
        widths, _ = split(columns)
        chunks = len(widths)
        vmem, smem = pl.BlockSpec(memory_space=pltpu.VMEM), pl.BlockSpec(memory_space=pltpu.SMEM)
        hbm = pl.BlockSpec(memory_space=pl.ANY)
        return pl.pallas_call(
            functools.partial(kernel, n_alpha, n_beta, rounds, chunks),
            out_shape=pltpu.VMEM((rows, columns), jnp.float32),
            in_specs=[smem, smem, vmem, hbm, hbm],
            out_specs=vmem,
            scratch_shapes=[
                pltpu.VMEM((rows, n_alpha * order), jnp.bfloat16),
                pltpu.VMEM((n_alpha * order, max(widths)), jnp.bfloat16),
                pltpu.VMEM(beta_tiles.shape, jnp.bfloat16),
                [pltpu.VMEM((n_alpha, n_blocks, order, width), jnp.bfloat16) for width in widths],
                [pltpu.VMEM((n_stops, rows, width), jnp.bfloat16) for width in widths],
                pltpu.SemaphoreType.DMA((chunks, n_alpha)),
                pltpu.SemaphoreType.DMA((chunks, n_alpha)),
                pltpu.SemaphoreType.DMA((chunks,)),
                pltpu.SemaphoreType.DMA((chunks, n_stops - 1)),
                pltpu.SemaphoreType.DMA((chunks, n_stops - 1)),
                pltpu.SemaphoreType.DMA(()),
            ],
            compiler_params=pltpu.CompilerParams(
                collective_id=0, has_side_effects=True, vmem_limit_bytes=48 * 2**20
            ),
        )(
            exc_list.transpose(2, 0, 1),
            counts,
            couplings,
            coefficients.reshape(n_blocks, order, columns),
            beta_tiles,
        )

    placed = (P("alpha", "beta"), P(), P(), P(), P(None, None, "beta"))
    return jax.shard_map(
        per_device, mesh=mesh, in_specs=placed, out_specs=P("alpha", "beta"), check_vma=False
    )
```
